128 devices in a mesh: seq: 32 (over z, y, core), fsdp: 4 (over x).
Axes of the slice: x: 4, y: 4, z: 4, core: 2. Of those that a mesh axis runs over, the one named last changes fastest.
Arguments:
- self_query: bfloat16 [4, 8192, 2048], P('fsdp', 'seq'), may hold values from -8 to 8, as said below
- self_key: bfloat16 [4, 8192, 2048], P('fsdp', 'seq'), may hold values from -8 to 8, as said below
- self_value: bfloat16 [4, 8192, 2048], P('fsdp', 'seq'), may hold values from -6 to 6
- cross_query: bfloat16 [4, 8192, 2048], P('fsdp', 'seq'), may hold values from -6 to 6
- neighbours: bfloat16 [4, 128, 256, 768], P('fsdp', 'seq'), may hold values from -6 to 6
- neighbour_count: int32 [4, 128], P('fsdp', 'seq'), may hold values from 1 to 2
- kv_weight: bfloat16 [768, 4096], P('fsdp'), may hold values from -0.21875 to 0.21875
- out_grad: bfloat16 [4, 8192, 2048], P('fsdp', 'seq'), may hold values from -6 to 6
Outputs:
- block_out: bfloat16 [4, 8192, 2048], P('fsdp', 'seq')
- query_grad: bfloat16 [4, 8192, 2048], P('fsdp', 'seq')
- key_grad: bfloat16 [4, 8192, 2048], P('fsdp', 'seq')
- value_grad: bfloat16 [4, 8192, 2048], P('fsdp', 'seq')
- cross_grad: bfloat16 [4, 8192, 2048], P('fsdp', 'seq')
- weight_grad: float32 [768, 4096], P(('seq', 'fsdp'))
The draws below stay inside these ranges and needn't reach their ends.
Inputs may be any that keep to these rules, and one draw needn't show every extreme that they name: `self_query`: entries of order one. `self_key`: entries of order one.
All inputs are finite; a program needn't handle non-finite values.
Results may differ from the reference program's by a relative error of at most 0.014.
Values may be sent and summed in bfloat16 or wider, within the bound.
A program may use at most 192 MiB of HBM per device.

```python
import jax
import jax.numpy as jnp
from jax import lax

HEADS = 16
HD = 128
ENC = 768
GROUP = 64
NEIGH = 2
RLEN = 128
HW = 2048
NB = 256
WINDOW = 256
FILES = 4
SEQ_LEN = 8192
GROUPS = 128


def draw_self_query(key, part):
    values_drawn = jnp.clip(jax.random.normal(jax.random.fold_in(key, 1), (FILES, SEQ_LEN, HW), jnp.float32), -6.0, 6.0)
    return values_drawn.astype(jnp.bfloat16)


def draw_self_key(key, part):
    values_drawn = jnp.clip(jax.random.normal(jax.random.fold_in(key, 2), (FILES, SEQ_LEN, HW), jnp.float32), -6.0, 6.0)
    return values_drawn.astype(jnp.bfloat16)


def set_ends(values, own_key, least, high):
    longest = values.shape.index(max(values.shape))
    spots = []
    for shift in (0, 1):
        where = [jax.random.randint(jax.random.fold_in(own_key, axis), (), 0, length) for axis, length in enumerate(values.shape)]
        where[longest] = (where[longest] + shift) % values.shape[longest]
        spots.append(tuple(where))
    return values.at[spots[0]].set(least).at[spots[1]].set(high)


def with_spikes(entries, stream_key, source, target, shards_of, factor):
    def block_of(dim):
        return (jnp.arange(entries.shape[dim]) // (entries.shape[dim] // shards_of)).reshape((-1,) + (1,) * (entries.ndim - 1 - dim))

    one_side = jax.random.permutation(stream_key, shards_of)[block_of(target)]
    second = (block_of(target) + shards_of // 2) % shards_of
    return jnp.where((block_of(source) == one_side) | (block_of(source) == second), factor * entries, entries)


def levels(rng, shape, pieces, least, top_value):
    factor_of, own = 1.0, jax.random.fold_in(rng, 6)
    for axis_at, parts in pieces:
        draws = jnp.exp(jax.random.uniform(jax.random.fold_in(own, axis_at), (parts,), jnp.float32, least / len(pieces), top_value / len(pieces)))
        factor_of = factor_of * jnp.repeat(draws, shape[axis_at] // parts).reshape([-1 if axis == axis_at else 1 for axis in range(len(shape))])
    return factor_of


def centred(key, dims, deviation, most, cuts=(), kind=jnp.bfloat16):
    gain = levels(key, dims, cuts, -0.22, 0.18) if cuts else 1.0
    drawn = jax.random.normal(key, dims, jnp.float32) * deviation * gain
    return jnp.minimum(jnp.maximum(drawn, -most), most).astype(kind)


def gaussian_with(rng, extent, width, most, pieces, heavy, kind=jnp.bfloat16):
    entries = width * jax.random.normal(rng, extent, jnp.float32)
    if pieces:
        entries = entries * levels(rng, extent, pieces, -0.22, 0.18)
    return jnp.clip(with_spikes(entries, jax.random.fold_in(rng, 3), *heavy), -most, most).astype(kind)


def setup_inputs(seed: int = 0) -> dict:
    seeds = jax.random.split(jax.random.key(seed), 9)
    self_query = draw_self_query(jax.random.fold_in(seeds[8], 71), 0)
    self_key = draw_self_key(jax.random.fold_in(seeds[8], 71), 0)
    self_value = centred(seeds[2], (FILES, SEQ_LEN, HW), 1.0, 6.0, ((0, 4), (1, 32)))
    cross_query = centred(seeds[3], (FILES, SEQ_LEN, HW), 1.0, 6.0, ((0, 4), (1, 32)))
    neighbours = gaussian_with(seeds[4], (FILES, GROUPS, NB, ENC), 1.0, 6.0, ((0, 4), (1, 32)), (1, 3, 32, 2.75))
    neighbour_count = set_ends(jax.random.randint(seeds[5], (FILES, GROUPS), 1, NEIGH + 1), jax.random.fold_in(seeds[5], 1), 1, NEIGH).astype(jnp.int32)
    kv_weight = centred(seeds[6], (ENC, 2 * HW), ENC ** -0.5, 0.21875, ((0, 4),))
    out_grad = centred(seeds[7], (FILES, SEQ_LEN, HW), 1.0, 6.0, ((0, 4), (1, 32)))
    return {"self_query": self_query, "self_key": self_key, "self_value": self_value, "cross_query": cross_query, "neighbours": neighbours, "neighbour_count": neighbour_count, "kv_weight": kv_weight, "out_grad": out_grad}


neg_fill = -1e30


def attend(queries, keys_in, values_in, grads, allowed, scaling):
    query_full = queries.astype(jnp.float32)
    key_full = keys_in.astype(jnp.float32)
    value_full = values_in.astype(jnp.float32)
    grad_full = grads.astype(jnp.float32)
    scores = jnp.einsum("...qhd,...khd->...hqk", query_full, key_full) * scaling
    scores = jnp.where(allowed, scores, neg_fill)
    peaks = jnp.max(scores, axis=-1, keepdims=True)
    weights = jnp.exp(scores - peaks)
    probs = weights / jnp.sum(weights, axis=-1, keepdims=True)
    probs_low = lax.optimization_barrier(probs.astype(jnp.bfloat16)).astype(jnp.float32)
    output = jnp.einsum("...hqk,...khd->...qhd", probs_low, value_full)
    prob_grad = jnp.einsum("...qhd,...khd->...hqk", grad_full, value_full)
    row_delta = jnp.sum(probs * prob_grad, axis=-1, keepdims=True)
    score_grad = lax.optimization_barrier((probs * (prob_grad - row_delta) * scaling).astype(jnp.bfloat16)).astype(jnp.float32)
    query_grad = jnp.einsum("...hqk,...khd->...qhd", score_grad, key_full)
    key_grad = jnp.einsum("...hqk,...qhd->...khd", score_grad, query_full)
    value_grad = jnp.einsum("...hqk,...qhd->...khd", probs_low, grad_full)
    return output, query_grad, key_grad, value_grad


def self_file(query_file, key_file, value_file, grad_file):
    tok_rows = WINDOW
    blocks = SEQ_LEN // tok_rows
    scaling = HD ** -0.5

    def blocked(array):
        return array.reshape(blocks, tok_rows, HEADS, HD)

    zero_block = jnp.zeros((1, tok_rows, HEADS, HD), jnp.bfloat16)
    key_blocks = blocked(key_file)
    value_blocks = blocked(value_file)
    key_before = jnp.concatenate([zero_block, key_blocks[:-1]], 0)
    value_before = jnp.concatenate([zero_block, value_blocks[:-1]], 0)
    row_index = jnp.arange(tok_rows, dtype=jnp.int32)[:, None]
    col_index = jnp.arange(2 * tok_rows, dtype=jnp.int32)[None, :]

    def one_block(inputs):
        query_block, key_prev, key_own, value_prev, value_own, grad_block, block_id = inputs
        allowed = (col_index > row_index) & (col_index <= row_index + tok_rows) & ((col_index >= tok_rows) | (block_id > 0))
        return attend(query_block, jnp.concatenate([key_prev, key_own], 0), jnp.concatenate([value_prev, value_own], 0), grad_block, allowed[None], scaling)

    output, query_grad, key_terms, value_terms = lax.map(one_block, (blocked(query_file), key_before, key_blocks, value_before, value_blocks, blocked(grad_file), jnp.arange(blocks, dtype=jnp.int32)))
    zero_terms = jnp.zeros((1, tok_rows, HEADS, HD), jnp.float32)
    key_grad = key_terms[:, tok_rows:] + jnp.concatenate([key_terms[1:, :tok_rows], zero_terms], 0)
    value_grad = value_terms[:, tok_rows:] + jnp.concatenate([value_terms[1:, :tok_rows], zero_terms], 0)
    return output.reshape(SEQ_LEN, HW), query_grad.reshape(SEQ_LEN, HW), key_grad.reshape(SEQ_LEN, HW), value_grad.reshape(SEQ_LEN, HW)


def cross_file(query_file, grad_file, neigh_file, count_file, kv_weight):
    neigh_rows = NEIGH * RLEN
    scaling = HD ** -0.5
    flat_neigh = neigh_file.reshape(GROUPS * neigh_rows, ENC)
    kv_proj = jnp.dot(flat_neigh, kv_weight, preferred_element_type=jnp.float32).astype(jnp.bfloat16).reshape(GROUPS, neigh_rows, 2 * HW)
    keys_all = kv_proj[..., :HW].reshape(GROUPS, neigh_rows, HEADS, HD)
    values_all = kv_proj[..., HW:].reshape(GROUPS, neigh_rows, HEADS, HD)
    key_before = jnp.concatenate([keys_all[:1], keys_all[:-1]], 0)
    value_before = jnp.concatenate([values_all[:1], values_all[:-1]], 0)
    count_before = jnp.concatenate([count_file[:1], count_file[:-1]], 0)
    neighbour_of = jnp.arange(neigh_rows, dtype=jnp.int32) // RLEN

    def one_group(inputs):
        query_group, grad_group, key_group, value_group, count_group, group_id = inputs
        allowed = (neighbour_of < count_group)[None, None, :]
        output, query_grad, key_grad, value_grad = attend(query_group, key_group, value_group, grad_group, allowed, scaling)
        live = group_id > 0
        output = jnp.where(live, output, 0.0)
        query_grad = jnp.where(live, query_grad, 0.0)
        kv_grad = jnp.concatenate([key_grad.reshape(neigh_rows, HW), value_grad.reshape(neigh_rows, HW)], -1)
        kv_grad = jnp.where(live, kv_grad, 0.0).astype(jnp.bfloat16)
        return output, query_grad, kv_grad

    group_view = (GROUPS, GROUP, HEADS, HD)
    output, query_grad, kv_grads = lax.map(one_group, (query_file.reshape(group_view), grad_file.reshape(group_view), key_before, value_before, count_before, jnp.arange(GROUPS, dtype=jnp.int32)))
    kv_grad_group = jnp.concatenate([kv_grads[1:], jnp.zeros((1, neigh_rows, 2 * HW), jnp.bfloat16)], 0)
    weight_part = jnp.dot(flat_neigh.T, kv_grad_group.reshape(GROUPS * neigh_rows, 2 * HW), preferred_element_type=jnp.float32)
    return output.reshape(SEQ_LEN, HW), query_grad.reshape(SEQ_LEN, HW), weight_part


def reference(self_query, self_key, self_value, cross_query, neighbours, neighbour_count, kv_weight, out_grad):
    def one_file(inputs):
        query_file, key_file, value_file, cross_file_q, neigh_file, count_file, grad_file = inputs
        self_out, query_grad, key_grad, value_grad = self_file(query_file, key_file, value_file, grad_file)
        cross_out, cross_grad, weight_part = cross_file(cross_file_q, grad_file, neigh_file, count_file, kv_weight)
        block_out = (self_out + cross_out).astype(jnp.bfloat16)
        return block_out, query_grad.astype(jnp.bfloat16), key_grad.astype(jnp.bfloat16), value_grad.astype(jnp.bfloat16), cross_grad.astype(jnp.bfloat16), weight_part

    block_out, query_grad, key_grad, value_grad, cross_grad, weight_parts = lax.map(one_file, (self_query, self_key, self_value, cross_query, neighbours, neighbour_count, out_grad))
    weight_grad = jnp.sum(weight_parts, axis=0)
    return (block_out, query_grad, key_grad, value_grad, cross_grad, weight_grad)
```

```python
import jax
import jax.numpy as jnp
from jax import lax
from jax.experimental import pallas as pl
from jax.experimental.pallas import tpu as pltpu
from jax.sharding import PartitionSpec as P

HEADS = 16
HD = 128
GROUP = 64
RLEN = 128
ROWS = 256
WIDTH = HEADS * HD
ENC = 768
SHARD = 192
SEQ = 32
FSDP = 4
NEG = -1e30
SCALE = HD ** -0.5
EXP_SCALE = SCALE * 1.4426950408889634
F32 = jnp.float32
BF16 = jnp.bfloat16
MESH = pl.DeviceIdType.MESH
PIECES = 4
PIECE = WIDTH // PIECES


def dot(a, b, contract):
    return lax.dot_general(a, b, (contract, ((), ())), preferred_element_type=F32)


def head_cols(h):
    return pl.ds(pl.multiple_of(h * HD, HD), HD)


def kernel(
    q_hbm, k_hbm, v_hbm, cq_hbm, nb_hbm, cnt_hbm, w_hbm, og_hbm,
    bo_hbm, qg_hbm, kg_hbm, vg_hbm, cg_hbm, wg_hbm,
    qb, ogb, cqb, kbuf, vbuf, so, qgb, kgb, vgb, cgb, bob,
    dps, dpr, dko, dvo, W, N4, NT, cown, cprev, mb, kvb, kvg,
    pbuf, r0, sb1, r1, sb2, r2, f3, sb3, own3, r3, wout,
    lsem, hs, hr, ns, nr, wos, wor, wfs, wfr, wps, wpr, dss, drr, osem,
    s0s, s0r, s1s, s1r, s2s, s2r, s3s, s3r,
):
    s = lax.axis_index("seq")
    x = lax.axis_index("fsdp")
    c = lax.rem(s, 2)
    y = lax.rem(lax.div(s, 2), 4)
    z = lax.div(s, 8)
    nxt = lax.rem(s + 1, SEQ)
    prv = lax.rem(s + SEQ - 1, SEQ)
    other = s + 1 - 2 * c
    xp = lax.rem(x + 1, FSDP)
    xm = lax.rem(x + FSDP - 1, FSDP)
    pri = z * (1 - c) + y * c
    sec = y * (1 - c) + z * c
    step1 = 8 * (1 - c) + 2 * c
    step2 = 2 * (1 - c) + 8 * c

    def remote(src, dst, send, recv, dev):
        return pltpu.make_async_remote_copy(
            src_ref=src, dst_ref=dst, send_sem=send, recv_sem=recv, device_id=dev, device_id_type=MESH
        )

    def shard_rows(at):
        return pl.ds(pl.multiple_of(at * SHARD, 16), SHARD)

    locals_in = [
        pltpu.make_async_copy(q_hbm, qb, lsem.at[0]),
        pltpu.make_async_copy(og_hbm, ogb, lsem.at[1]),
        pltpu.make_async_copy(k_hbm, kbuf.at[pl.ds(ROWS, ROWS)], lsem.at[2]),
        pltpu.make_async_copy(v_hbm, vbuf.at[pl.ds(ROWS, ROWS)], lsem.at[3]),
        pltpu.make_async_copy(cnt_hbm, cown, lsem.at[4]),
        pltpu.make_async_copy(nb_hbm.at[pl.ds(0, 768)], N4.at[pl.ds(256, 768)], lsem.at[5]),
        pltpu.make_async_copy(cq_hbm, cqb, lsem.at[6]),
        pltpu.make_async_copy(w_hbm, W.at[shard_rows(x)], lsem.at[7]),
    ]
    for copy in locals_in:
        copy.start()

    barrier = pltpu.get_barrier_semaphore()
    peers = [(nxt, x), (prv, x), (other, x)]
    for d in range(1, 4):
        peers.append((s + (lax.rem(pri + d, 4) - pri) * step1, x))
        peers.append((s + (lax.rem(sec + d, 4) - sec) * step2, x))
        peers.append((s, lax.rem(x + d, FSDP)))
        peers.append((other, lax.rem(x + d, FSDP)))
    for dev in peers:
        pl.semaphore_signal(barrier, inc=1, device_id=dev, device_id_type=MESH)

    first = s == 0
    for r in range(2):
        row = lax.broadcasted_iota(jnp.int32, (128, 384), 0)
        col = lax.broadcasted_iota(jnp.int32, (128, 384), 1)
        least = jnp.where(first, 256 - 128 * r, 0)
        ok = (col > row) & (col <= row + 256) & (col >= least)
        mb[r] = jnp.where(ok, 0.0, NEG)
    f3[...] = jnp.zeros_like(f3)

    pl.semaphore_wait(barrier, len(peers))

    def piece_cols(half, j):
        return pl.ds(pl.multiple_of(half * WIDTH + j * PIECE, PIECE), PIECE)

    def own_piece(j, side):
        dst = W.at[shard_rows(x), piece_cols(c, j)]
        return remote(w_hbm.at[:, piece_cols(c, j)], dst, wos.at[side, j], wor.at[side, j], (s, (xp, xm)[side]))

    def passed_on(j):
        side = 0 if j < PIECES // 2 else 1
        at = W.at[shard_rows((xm, xp)[side]), piece_cols(c, j)]
        return remote(at, at, wfs.at[j], wfr.at[j], (s, (xp, xm)[side]))

    def to_other(j, d):
        at = W.at[shard_rows(lax.rem(x + d, FSDP)), piece_cols(c, j)]
        return remote(at, at, wps.at[d - 1, j], wpr.at[d - 1, j], (other, x))

    def halo(h):
        cols = head_cols(h)
        return [
            remote(k_hbm.at[:, cols], kbuf.at[pl.ds(0, ROWS), cols], hs.at[0], hr.at[0, h], (nxt, x)),
            remote(v_hbm.at[:, cols], vbuf.at[pl.ds(0, ROWS), cols], hs.at[1], hr.at[1, h], (nxt, x)),
        ]

    halo_nb = remote(nb_hbm.at[pl.ds(768, 256)], N4.at[pl.ds(0, 256)], ns.at[0], nr.at[0], (nxt, x))
    halo_cnt = remote(cnt_hbm, cprev, ns.at[1], nr.at[1], (nxt, x))

    for j in range(2):
        for side in range(2):
            own_piece(j, side).start()

    @pl.loop(0, HEADS)
    def _(h):
        for copy in halo(h):
            copy.start()

    halo_nb.start()
    halo_cnt.start()

    for copy in locals_in[:4]:
        copy.wait()

    def grad_return(h):
        return remote(dps.at[h], dpr.at[h], dss.at[0], drr.at[h], (prv, x))

    def column_out(buf, hbm, at, h):
        return pltpu.make_async_copy(buf.at[:, head_cols(h)], hbm.at[:, head_cols(h)], osem.at[at])

    @pl.loop(0, HEADS)
    def _(h):
        cols = head_cols(h)
        for copy in halo(h):
            copy.wait_recv()
        dk = []
        dv = []
        for r in range(2):
            rows = pl.ds(128 * r, 128)
            span = pl.ds(128 * r, 384)
            q = qb[rows, cols]
            og = ogb[rows, cols]
            kk = kbuf[span, cols]
            vv = vbuf[span, cols]
            raw = dot(q, kk, ((1,), (1,))) + mb[r]
            e = jnp.exp2((raw - jnp.max(raw, axis=1, keepdims=True)) * EXP_SCALE)
            p = e * (1.0 / jnp.sum(e, axis=1, keepdims=True))
            low = p.astype(BF16)
            so[rows, cols] = dot(low, vv, ((1,), (0,)))
            gp = dot(og, vv, ((1,), (1,)))
            sg = (p * (gp - jnp.sum(p * gp, axis=1, keepdims=True))).astype(BF16)
            qgb[rows, cols] = (dot(sg, kk, ((1,), (0,))) * SCALE).astype(BF16)
            dk.append(dot(sg, q, ((0,), (0,))) * SCALE)
            dv.append(dot(low, og, ((0,), (0,))))
        column_out(qgb, qg_hbm, 1, h).start()
        for at, (terms, own) in enumerate(((dk, dko), (dv, dvo))):
            dps[h, at, 0:128] = terms[0][0:128].astype(BF16)
            dps[h, at, 128:256] = (terms[0][128:256] + terms[1][0:128]).astype(BF16)
            own[h, 0:128] = terms[0][256:384] + terms[1][128:256]
            own[h, 128:256] = terms[1][256:384]
        grad_return(h).start()

        @pl.when(h == 4)
        def _():
            own_piece(0, 0).wait_recv()
            own_piece(0, 1).wait_recv()
            passed_on(0).start()
            own_piece(2, 0).start()
            own_piece(2, 1).start()
            to_other(0, 3).start()
            to_other(0, 1).start()

        @pl.when(h == 7)
        def _():
            own_piece(1, 0).wait_recv()
            own_piece(1, 1).wait_recv()
            passed_on(1).start()
            own_piece(3, 0).start()
            own_piece(3, 1).start()
            to_other(1, 3).start()
            to_other(1, 1).start()

        @pl.when(h == 11)
        def _():
            own_piece(2, 0).wait_recv()
            own_piece(2, 1).wait_recv()
            passed_on(2).start()
            to_other(2, 3).start()
            to_other(2, 1).start()
            passed_on(0).wait_recv()
            to_other(0, 2).start()

        @pl.when(h == 14)
        def _():
            own_piece(3, 0).wait_recv()
            own_piece(3, 1).wait_recv()
            passed_on(3).start()
            to_other(3, 3).start()
            to_other(3, 1).start()
            passed_on(1).wait_recv()
            to_other(1, 2).start()

    for copy in locals_in[4:]:
        copy.wait()
    halo_nb.wait_recv()
    halo_cnt.wait_recv()
    NT[...] = N4[...].T

    def first_copy(h):
        return remote(pbuf.at[h, 1 - c], r0.at[h], s0s.at[0], s0r.at[h], (other, x))

    def second_copy(h, d):
        to = lax.rem(pri + d, 4)
        return remote(sb1.at[h, to], r1.at[h, d - 1], s1s.at[d - 1], s1r.at[h], (s + (to - pri) * step1, x))

    def third_copy(h, d):
        to = lax.rem(sec + d, 4)
        return remote(sb2.at[h, to], r2.at[h, d - 1], s2s.at[d - 1], s2r.at[h], (s + (to - sec) * step2, x))

    def last_copy(h, slot):
        if slot < 3:
            half, to, dev = c, lax.rem(x + slot + 1, FSDP), s
        else:
            half, to, dev = 1 - c, lax.rem(x + slot - 3, FSDP), other
        return remote(sb3.at[h, half * 4 + to], r3.at[h, slot], s3s.at[slot], s3r.at[h], (dev, to))

    def landed(ref, sem):
        return pltpu.make_async_copy(ref, ref, sem)

    @pl.loop(0, HEADS + 4)
    def _(t):
        @pl.when(t >= 4)
        def _():
            h = t - 4
            landed(r3.at[h], s3r.at[h]).wait()
            mine = own3[h] + r3[h, 0] + r3[h, 1] + r3[h, 2]
            theirs = r3[h, 3] + r3[h, 4] + r3[h, 5] + r3[h, 6]
            wout[:, pl.ds(pl.multiple_of(c * WIDTH + h * HD, HD), HD)] = mine[0:6]
            wout[:, pl.ds(pl.multiple_of((1 - c) * WIDTH + h * HD, HD), HD)] = theirs[0:6]

        @pl.when((t >= 3) & (t < HEADS + 3))
        def _():
            h = t - 3
            landed(r2.at[h], s2r.at[h]).wait()
            total = sb2[h, sec].astype(F32)
            for d in range(3):
                total += r2[h, d].astype(F32)
            f3[0:48] = total
            for to in range(8):
                sb3[h, to] = f3[pl.ds(6 * to, 8)]
            own3[h] = sb3[h, c * 4 + x]
            for slot in range(7):
                last_copy(h, slot).start()

        @pl.when((t >= 2) & (t < HEADS + 2))
        def _():
            h = t - 2
            landed(r1.at[h], s1r.at[h]).wait()
            total = sb1[h, pri].astype(F32)
            for d in range(3):
                total += r1[h, d].astype(F32)
            sb2[h] = total.astype(BF16)
            for d in range(1, 4):
                third_copy(h, d).start()

        @pl.when((t >= 1) & (t < HEADS + 1))
        def _():
            h = t - 1
            first_copy(h).wait_recv()
            for a in range(4):
                for b in range(4):
                    rows = pl.ds((a * 4 + b) * 48, 48)
                    total = pbuf[h, c, rows].astype(F32) + r0[h, rows].astype(F32)
                    sb1[h, a * (1 - c) + b * c, b * (1 - c) + a * c] = total.astype(BF16)
            for d in range(1, 4):
                second_copy(h, d).start()

        for j in range(PIECES):
            @pl.when(t == j * (HEADS // PIECES))
            def _():
                if j >= 2:
                    passed_on(j).wait_recv()
                    to_other(j, 2).start()
                for d in (1, 2, 3):
                    at = W.at[shard_rows(lax.rem(x + d, FSDP)), piece_cols(1 - c, j)]
                    landed(at, wpr.at[d - 1, j]).wait()

        @pl.when(t < HEADS)
        def _():
            h = t
            cols = head_cols(h)
            wh = jnp.concatenate([W[:, cols], W[:, head_cols(h + HEADS)]], axis=1)
            kvb[...] = dot(N4[...], wh, ((1,), (0,))).astype(BF16)
            for g in range(4):
                rows = pl.ds(GROUP * g, GROUP)
                span = pl.ds(256 * g, 256)
                q = cqb[rows, cols]
                og = ogb[rows, cols]
                kk = kvb[span, 0:HD]
                vv = kvb[span, HD : 2 * HD]
                count = cprev[3:4] if g == 0 else cown[g - 1 : g]
                bias = jnp.where(count >= 2.0, 0.0, NEG)
                bias = jnp.concatenate([jnp.zeros_like(bias), bias], axis=1)
                raw = dot(q, kk, ((1,), (1,))) + bias
                e = jnp.exp2((raw - jnp.max(raw, axis=1, keepdims=True)) * EXP_SCALE)
                inverse = 1.0 / jnp.sum(e, axis=1, keepdims=True)
                if g == 0:
                    inverse = inverse * jnp.where(first, 0.0, 1.0)
                p = e * inverse
                low = p.astype(BF16)
                out = dot(low, vv, ((1,), (0,)))
                bob[rows, cols] = (so[rows, cols] + out).astype(BF16)
                gp = dot(og, vv, ((1,), (1,)))
                sg = (p * (gp - jnp.sum(p * gp, axis=1, keepdims=True))).astype(BF16)
                cgb[rows, cols] = (dot(sg, kk, ((1,), (0,))) * SCALE).astype(BF16)
                kvg[span, 0:HD] = (dot(sg, q, ((0,), (0,))) * SCALE).astype(BF16)
                kvg[span, HD : 2 * HD] = dot(low, og, ((0,), (0,))).astype(BF16)
            part = dot(NT[...], kvg[...], ((1,), (0,)))
            pbuf[h, 0] = part[:, 0:HD].astype(BF16)
            pbuf[h, 1] = part[:, HD : 2 * HD].astype(BF16)
            first_copy(h).start()
            column_out(bob, bo_hbm, 0, h).start()
            column_out(cgb, cg_hbm, 4, h).start()
            grad_return(h).wait_recv()
            kgb[:, cols] = (dko[h] + dpr[h, 0].astype(F32)).astype(BF16)
            vgb[:, cols] = (dvo[h] + dpr[h, 1].astype(F32)).astype(BF16)
            column_out(kgb, kg_hbm, 2, h).start()
            column_out(vgb, vg_hbm, 3, h).start()

    weight_out = pltpu.make_async_copy(wout, wg_hbm, osem.at[5])
    weight_out.start()
    remote(k_hbm, kbuf.at[pl.ds(0, ROWS)], hs.at[0], hr.at[0, 0], (nxt, x)).wait_send()
    remote(v_hbm, vbuf.at[pl.ds(0, ROWS)], hs.at[1], hr.at[1, 0], (nxt, x)).wait_send()
    halo_nb.wait_send()
    halo_cnt.wait_send()
    for j in range(PIECES):
        own_piece(j, 0).wait_send()
        own_piece(j, 1).wait_send()
        passed_on(j).wait_send()
        for d in (1, 2, 3):
            to_other(j, d).wait_send()
    landed(dps, dss.at[0]).wait()
    landed(r0, s0s.at[0]).wait()
    for d in range(3):
        landed(r1.at[:, d], s1s.at[d]).wait()
        landed(r2.at[:, d], s2s.at[d]).wait()
    for slot in range(7):
        landed(r3.at[:, slot], s3s.at[slot]).wait()
    for at, (buf, hbm) in enumerate(((bob, bo_hbm), (qgb, qg_hbm), (kgb, kg_hbm), (vgb, vg_hbm), (cgb, cg_hbm))):
        pltpu.make_async_copy(buf, hbm, osem.at[at]).wait()
    weight_out.wait()


def on_device(
    self_query, self_key, self_value, cross_query, neighbours, neighbour_count, kv_weight, out_grad
):
    counts = jnp.zeros((8, 128), F32) + jnp.pad(neighbour_count[0].astype(F32), (0, 4))[:, None]
    wide = jax.ShapeDtypeStruct((ROWS, WIDTH), BF16)
    token = lambda dtype=BF16: pltpu.VMEM((ROWS, WIDTH), dtype)
    dma = lambda *shape: pltpu.SemaphoreType.DMA(shape)
    anywhere = pl.BlockSpec(memory_space=pl.ANY)
    outs = pl.pallas_call(
        kernel,
        out_shape=[wide] * 5 + [jax.ShapeDtypeStruct((6, 2 * WIDTH), F32)],
        in_specs=[anywhere] * 8,
        out_specs=[anywhere] * 6,
        scratch_shapes=[
            token(), token(), token(),
            pltpu.VMEM((2 * ROWS, WIDTH), BF16), pltpu.VMEM((2 * ROWS, WIDTH), BF16),
            token(F32), token(), token(), token(), token(), token(),
            pltpu.VMEM((HEADS, 2, ROWS, HD), BF16), pltpu.VMEM((HEADS, 2, ROWS, HD), BF16),
            pltpu.VMEM((HEADS, ROWS, HD), F32), pltpu.VMEM((HEADS, ROWS, HD), F32),
            pltpu.VMEM((ENC, 2 * WIDTH), BF16), pltpu.VMEM((1024, ENC), BF16), pltpu.VMEM((ENC, 1024), BF16),
            pltpu.VMEM((8, 128), F32), pltpu.VMEM((8, 128), F32),
            pltpu.VMEM((2, 128, 384), F32),
            pltpu.VMEM((1024, 2 * HD), BF16), pltpu.VMEM((1024, 2 * HD), BF16),
            pltpu.VMEM((HEADS, 2, ENC, HD), BF16), pltpu.VMEM((HEADS, ENC, HD), BF16),
            pltpu.VMEM((HEADS, 4, 4, 48, HD), BF16), pltpu.VMEM((HEADS, 3, 4, 48, HD), BF16),
            pltpu.VMEM((HEADS, 4, 48, HD), BF16), pltpu.VMEM((HEADS, 3, 48, HD), BF16),
            pltpu.VMEM((56, HD), F32), pltpu.VMEM((HEADS, 8, 8, HD), F32),
            pltpu.VMEM((HEADS, 8, HD), F32), pltpu.VMEM((HEADS, 7, 8, HD), F32),
            pltpu.VMEM((6, 2 * WIDTH), F32),
            dma(8), dma(2), dma(2, HEADS), dma(2), dma(2),
            dma(2, PIECES), dma(2, PIECES), dma(PIECES), dma(PIECES), dma(3, PIECES), dma(3, PIECES),
            dma(1), dma(HEADS), dma(6),
            dma(1), dma(HEADS), dma(3), dma(HEADS), dma(3), dma(HEADS), dma(7), dma(HEADS),
        ],
        compiler_params=pltpu.CompilerParams(
            collective_id=0, has_side_effects=True, vmem_limit_bytes=67043328
        ),
    )(
        self_query[0], self_key[0], self_value[0], cross_query[0], neighbours.reshape(1024, ENC),
        counts, kv_weight, out_grad[0],
    )
    return tuple(array[None] for array in outs[:5]) + (outs[5],)


def solution(mesh):
    wide = P("fsdp", "seq", None)
    return jax.shard_map(
        on_device,
        mesh=mesh,
        in_specs=(wide, wide, wide, wide, P("fsdp", "seq", None, None), P("fsdp", "seq"), P("fsdp", None), wide),
        out_specs=(wide, wide, wide, wide, wide, P(("seq", "fsdp"), None)),
        check_vma=False,
    )
```
